256 devices in a mesh: user: 8 (over x, core), item: 32 (over y, z).
Axes of the slice: x: 4, y: 4, z: 8, core: 2. Of those that a mesh axis runs over, the one named last changes fastest.
Arguments:
- user_factors: float32 [65536, 256], P(('user', 'item')), may hold values from -6 to 6
- item_factors: bfloat16 [131072, 256], P('item')
- head_ids: int32 [8], replicated, may hold values from 0 to 511, as said below
- tail_ids: int32 [256, 16], P(('user', 'item')), may hold values from 0 to 511, as said below
- head_counts: int32 [256, 8, 256, 256], P(('user', 'item')), may hold values from 0 to 7
- tail_counts: int32 [256, 16, 256, 256], P(('user', 'item')), may hold values from 0 to 7
Outputs:
- new_factors: float32 [65536, 256], P(('user', 'item'))
- residual: float32 [65536, 256], P(('user', 'item'))
The draws below stay inside these ranges and needn't reach their ends.
Inputs may be any that keep to these rules, and one draw needn't show every extreme that they name: `head_ids`: 8 distinct block numbers, among them 0 and 511. `tail_ids`: each row holds distinct block numbers; at most 1 of a row fall in the range of one index of item (blocks o * 16 to (o + 1) * 16 - 1), and one range, the same for every row, holds exactly 1 of every row.
All inputs are finite; a program needn't handle non-finite values.
Results may differ from the reference program's by a relative error of at most 0.0055.
Values may be sent and summed in bfloat16 or wider, within the bound.
No kernel may reach another device: no remote copies, remote signals or barrier semaphores. Data moves between devices by JAX's collectives and lax.ppermute only.
A program may use at most 128 MiB of HBM per device.

```python
import math
import jax
import jax.numpy as jnp
from jax import lax

F = 256
BLK = 256
ITERS = 2
HEAD_B = 8
TAIL_K = 16
NUM_ITEMS = 131072
SHARD_BLOCKS = 16
ITEM_BLOCKS = 512
CAP = 1
USER_BLOCKS = 256
USERS = 65536


def draw_item_factors(key, part):
    key_col, key_row, key_noise = jax.random.split(key, 3)
    column_scale = jnp.exp(jax.random.uniform(key_col, (1, F), minval=math.log(0.3), maxval=math.log(3.0)))
    row_scale = jnp.exp(jax.random.uniform(key_row, (NUM_ITEMS, 1), minval=0.0, maxval=math.log(3.0)))
    position = jnp.arange(NUM_ITEMS, dtype=jnp.float32).reshape(NUM_ITEMS, 1)
    row_scale = row_scale * (1.0 + 2.0 * position / NUM_ITEMS)
    noise = jax.random.normal(key_noise, (NUM_ITEMS, F))
    values = noise * column_scale * row_scale / math.sqrt(NUM_ITEMS)
    return values.astype(jnp.float32).astype(jnp.bfloat16)


def draw_head_ids(key, part):
    key_pick, key_order = jax.random.split(jax.random.fold_in(key, 3))
    middle = jax.random.permutation(key_pick, ITEM_BLOCKS - 2)[:HEAD_B - 2] + 1
    ends = jnp.array([0, ITEM_BLOCKS - 1], dtype=jnp.int32)
    chosen = jnp.concatenate([ends, middle.astype(jnp.int32)])
    return chosen[jax.random.permutation(key_order, HEAD_B)].astype(jnp.int32)


def draw_tail_ids(key, part):
    hot_key, rest_key = jax.random.split(jax.random.fold_in(key, 7))
    owner_total = ITEM_BLOCKS // SHARD_BLOCKS
    slot_total = owner_total * CAP
    hot_owner = jax.random.randint(hot_key, (), 0, owner_total)

    def draw_row(row_key):
        key_order, key_band, key_shuffle = jax.random.split(row_key, 3)
        order_rank = jax.random.permutation(key_order, slot_total)
        slot_owner = jnp.arange(slot_total) // CAP
        score_int = jnp.where(slot_owner == hot_owner, 0, 1) * slot_total + order_rank
        chosen = jnp.argsort(score_int)[:TAIL_K]
        pick_owner = chosen // CAP
        within = chosen % CAP
        band_index = jax.random.randint(key_band, (TAIL_K,), 0, SHARD_BLOCKS // CAP)
        block_ids = pick_owner * SHARD_BLOCKS + band_index * CAP + within
        return block_ids[jax.random.permutation(key_shuffle, TAIL_K)]
    row_keys = jax.random.split(rest_key, USER_BLOCKS)
    return jax.vmap(draw_row)(row_keys).astype(jnp.int32)


def plant(values, rng, least, top_value):
    index_at = [jax.random.randint(jax.random.fold_in(rng, axis), (), 0, length) for axis, length in enumerate(values.shape)]
    widest = values.shape.index(max(values.shape))
    neighbour = index_at[:widest] + [(index_at[widest] + 1) % values.shape[widest]] + index_at[widest + 1:]
    return values.at[tuple(index_at)].set(least).at[tuple(neighbour)].set(top_value)


def block_levels(rng, shape, shards, smallest, largest):
    level = 1.0
    for dim, parts in shards:
        steps = jax.random.uniform(jax.random.fold_in(jax.random.fold_in(rng, 6), dim), (parts,), jnp.float32, smallest / len(shards), largest / len(shards))
        level = level * jnp.repeat(jnp.exp(steps), shape[dim] // parts).reshape((-1,) + (1,) * (len(shape) - 1 - dim))
    return level


def scatter_about(key, extent, spread, limit, cuts=(), kind=jnp.bfloat16):
    entries = jax.random.normal(key, extent, jnp.float32) * spread
    if len(cuts) > 0:
        entries = block_levels(key, extent, cuts, -0.22, 0.18) * entries
    return jnp.clip(entries, min=-limit, max=limit).astype(kind)


def setup_inputs(seed: int = 0) -> dict:
    key_of = jax.random.split(jax.random.key(seed), 7)
    user_factors = scatter_about(key_of[0], (USERS, F), 1.0, 6.0, ((0, 256),), jnp.float32)
    item_factors = draw_item_factors(jax.random.fold_in(key_of[6], 71), 0)
    head_ids = draw_head_ids(jax.random.fold_in(key_of[6], 71), 0)
    tail_ids = draw_tail_ids(jax.random.fold_in(key_of[6], 71), 0)
    head_counts = plant(jax.random.randint(key_of[4], (USER_BLOCKS, HEAD_B, BLK, BLK), 0, 8), jax.random.fold_in(key_of[4], 1), 0, 7).astype(jnp.int32)
    tail_counts = plant(jax.random.randint(key_of[5], (USER_BLOCKS, TAIL_K, BLK, BLK), 0, 8), jax.random.fold_in(key_of[5], 1), 0, 7).astype(jnp.int32)
    return {"user_factors": user_factors, "item_factors": item_factors, "head_ids": head_ids, "tail_ids": tail_ids, "head_counts": head_counts, "tail_counts": tail_counts}


conf_alpha = 4.0
ridge_term = 0.1
epsilon = 1e-6


def apply_operator(vector, gram_matrix, item_tiles, weights):
    rounded = vector.astype(jnp.bfloat16)
    scores = jnp.einsum('uf,kif->kui', rounded.astype(jnp.float32), item_tiles.astype(jnp.float32))
    scaled = (scores * weights.astype(jnp.float32)).astype(jnp.bfloat16)
    data_term = jnp.einsum('kui,kif->uf', scaled.astype(jnp.float32), item_tiles.astype(jnp.float32))
    gram_term = jnp.dot(vector, gram_matrix, precision=lax.Precision.HIGHEST)
    return gram_term + ridge_term * vector + data_term


def solve_block(start_vec, gram_matrix, item_tiles, counts):
    count_float = counts.astype(jnp.float32)
    weights = (conf_alpha * count_float).astype(jnp.bfloat16)
    rated_weight = jnp.where(counts > 0, 1.0 + conf_alpha * count_float, 0.0).astype(jnp.bfloat16)
    rhs = jnp.einsum('kui,kif->uf', rated_weight.astype(jnp.float32), item_tiles.astype(jnp.float32))
    solution = start_vec
    residual = rhs - apply_operator(solution, gram_matrix, item_tiles, weights)
    direction = residual
    norm_now = jnp.sum(residual * residual, axis=1, keepdims=True)
    for turn_index in range(ITERS):
        image_vec = apply_operator(direction, gram_matrix, item_tiles, weights)
        step_size = norm_now / (jnp.sum(direction * image_vec, axis=1, keepdims=True) + epsilon)
        solution = solution + step_size * direction
        residual = residual - step_size * image_vec
        if turn_index + 1 < ITERS:
            norm_next = jnp.sum(residual * residual, axis=1, keepdims=True)
            direction = residual + (norm_next / (norm_now + epsilon)) * direction
            norm_now = norm_next
    return solution, residual


def reference(user_factors, item_factors, head_ids, tail_ids, head_counts, tail_counts):
    gram_matrix = jnp.dot(item_factors.T, item_factors, preferred_element_type=jnp.float32)
    blocks = item_factors.reshape(ITEM_BLOCKS, BLK, F)
    head_rows = blocks[head_ids]

    def one_block(block_args):
        start_vec, tail_list, head_part, tail_part = block_args
        item_tiles = jnp.concatenate([head_rows, blocks[tail_list]], axis=0)
        counts = jnp.concatenate([head_part, tail_part], axis=0)
        return solve_block(start_vec, gram_matrix, item_tiles, counts)

    user_blocks = user_factors.reshape(USER_BLOCKS, BLK, F)
    solution, residual = lax.map(one_block, (user_blocks, tail_ids, head_counts, tail_counts))
    return solution.reshape(USERS, F), residual.reshape(USERS, F)
```

```python
import jax
import jax.numpy as jnp
from jax import lax
from jax.experimental import pallas as pl
from jax.experimental.pallas import tpu as pltpu
from jax.sharding import Mesh, PartitionSpec as P

ITERS = 2

conf_alpha = 4.0
ridge_term = 0.1
epsilon = 1e-06

USER, Y_SIZE, Z_SIZE = 8, 4, 8
ALL = ("user", "y", "z")
PLANE = ("user", "y")
NEAR = (0, -1, 1)
FAR = (-2, 2, -3, 3, 4)
SLOT_OF_SHIFT = tuple((NEAR + FAR).index(s if s <= 4 else s - 8) for s in range(8))


def whole(array):
    return pl.BlockSpec(array.shape, lambda *_: (0,) * len(array.shape))


def bf16(*shape):
    return jax.ShapeDtypeStruct(shape, jnp.bfloat16)


def store_split(out, at, values):
    high = values.astype(jnp.bfloat16)
    out[at] = high
    out[at + 1] = (values - high.astype(jnp.float32)).astype(jnp.bfloat16)


def prepare_kernel(place, blocks, out, gram):
    total, block, width = blocks.shape
    band = block // USER
    row = pl.multiple_of(place[0] * band, band)
    for k in range(total):
        rows = blocks[k]
        part = lax.dot_general(rows, rows, (((0,), (0,)), ((), ())), preferred_element_type=jnp.float32)
        if k == 0:
            gram[...] = part
        else:
            gram[...] += part
        out[k] = blocks[k, pl.ds(row, band), :]
    store_split(out, total, gram[pl.ds(row, width // USER), :])


def prepare(blocks, user):
    total, block, width = blocks.shape
    out = bf16(total + 2, block // USER, width)
    return pl.pallas_call(
        prepare_kernel,
        name="prepare",
        grid_spec=pltpu.PrefetchScalarGridSpec(
            num_scalar_prefetch=1,
            grid=(1,),
            in_specs=[whole(blocks)],
            out_specs=whole(out),
            scratch_shapes=[pltpu.VMEM((width, width), jnp.float32)],
        ),
        out_shape=out,
    )(user.reshape(1), blocks)


def pick_near_kernel(wanted, place, own, down, up, out):
    z = place[0]
    band = own.shape[1]
    peers = out.shape[0]
    first = pl.program_id(0) * peers
    for p in range(peers):
        for slot, (source, offset) in enumerate(zip((own, down, up), NEAR)):
            out[p, slot * band : (slot + 1) * band, :] = source[wanted[first + p, (z + offset) & (Z_SIZE - 1)]]


def pick_near(wanted, z, pieces):
    _, band, width = pieces[0].shape
    out = bf16(wanted.shape[0], len(NEAR) * band, width)
    return pl.pallas_call(
        pick_near_kernel,
        name="pick_near",
        grid_spec=pltpu.PrefetchScalarGridSpec(
            num_scalar_prefetch=2,
            grid=(2,),
            in_specs=[whole(piece) for piece in pieces],
            out_specs=pl.BlockSpec((out.shape[0] // 2, *out.shape[1:]), lambda i, *_: (i, 0, 0)),
        ),
        out_shape=out,
    )(wanted, z.reshape(1), *pieces)


def pick_far_kernel(wanted, head_ids, place, *refs):
    pieces, (out, shared) = refs[:-2], refs[-2:]
    z = place[0]
    total, band, width = pieces[0].shape
    per_shard = total - 2
    heads = head_ids.shape[0]
    peers = out.shape[0]
    first = pl.program_id(0) * peers

    @pl.when(pl.program_id(0) == 0)
    def _():
        def one_head(h, carry):
            block = head_ids[h]
            shift = (block // per_shard - z) & (Z_SIZE - 1)
            for source, offset in zip(pieces, NEAR + FAR):

                @pl.when(shift == offset % Z_SIZE)
                def _():
                    shared[h] = source[block & (per_shard - 1)]

            return carry

        lax.fori_loop(0, heads, one_head, 0)
        gram = jnp.zeros((band, width), jnp.float32)
        for source in pieces:
            gram += source[per_shard].astype(jnp.float32) + source[per_shard + 1].astype(jnp.float32)
        store_split(shared, heads, gram)

    for p in range(peers):
        for slot, (source, offset) in enumerate(zip(pieces[len(NEAR) :], FAR)):
            out[p, slot * band : (slot + 1) * band, :] = source[wanted[first + p, (z + offset) & (Z_SIZE - 1)]]


def pick_far(wanted, head_ids, z, pieces):
    _, band, width = pieces[0].shape
    out = bf16(wanted.shape[0], len(FAR) * band, width)
    shared = bf16(head_ids.shape[0] + 2, band, width)
    return pl.pallas_call(
        pick_far_kernel,
        name="pick_far",
        grid_spec=pltpu.PrefetchScalarGridSpec(
            num_scalar_prefetch=3,
            grid=(4,),
            in_specs=[whole(piece) for piece in pieces],
            out_specs=(
                pl.BlockSpec((out.shape[0] // 4, *out.shape[1:]), lambda i, *_: (i, 0, 0)),
                whole(shared),
            ),
        ),
        out_shape=(out, shared),
    )(wanted, head_ids, z.reshape(1), *pieces)


def merge_kernel(slabs, place, own, above, across, below, out):
    heads = slabs.shape[0]
    pieces = (own, above, across, below)
    for h in range(heads):
        shift = (slabs[h] - place[0]) & (Y_SIZE - 1)
        for other, source in enumerate(pieces):

            @pl.when(shift == other)
            def _():
                out[h] = source[h]

    gram = jnp.zeros(out.shape[1:], jnp.float32)
    for source in pieces:
        gram += source[heads].astype(jnp.float32) + source[heads + 1].astype(jnp.float32)
    store_split(out, heads, gram)


def merge(slabs, y, pieces):
    return pl.pallas_call(
        merge_kernel,
        name="merge",
        grid_spec=pltpu.PrefetchScalarGridSpec(
            num_scalar_prefetch=2,
            grid=(1,),
            in_specs=[whole(piece) for piece in pieces],
            out_specs=whole(pieces[0]),
        ),
        out_shape=bf16(*pieces[0].shape),
    )(slabs, y.reshape(1), *pieces)


def solve_kernel(slab, slot, place, start, near, far, same, other, head_counts, tail_counts, new_out, res_out, tiles, weights, counts, halves, gram, acc, tile_sems, count_sems, gram_sems, head_sems):
    heads, tails = head_counts.shape[1], tail_counts.shape[1]
    total = heads + tails
    block, width = start.shape
    band = same.shape[2]

    gram_copies, head_copies = [], []
    x, core = place[0] // 2, place[0] % 2
    for i, source in enumerate((same, other)):
        for j in range(USER // 2):
            n = i * (USER // 2) + j
            user = ((x + j) & (USER // 2 - 1)) * 2 + (core if i == 0 else 1 - core)
            gram_copies.append(pltpu.make_async_copy(source.at[j, heads:], halves.at[:, user], gram_sems.at[n]))
            head_copies.append(pltpu.make_async_copy(source.at[j, :heads], tiles.at[:heads, user], head_sems.at[n]))
    count_copies = [pltpu.make_async_copy(head_counts.at[0, k], counts.at[k], count_sems.at[k]) for k in range(heads)]
    count_copies += [
        pltpu.make_async_copy(tail_counts.at[0, k], counts.at[heads + k], count_sems.at[heads + k]) for k in range(tails)
    ]

    def tail_copy(k, source, first, any_rows=False):
        row = 0 if any_rows else pl.multiple_of((slot[k] - first) * band, band)
        return pltpu.make_async_copy(
            source.at[:, 0 if any_rows else slab[k], pl.ds(row, band), :], tiles.at[heads + k], tile_sems.at[heads + k]
        )

    for copy in gram_copies:
        copy.start()
    for k in range(tails):

        @pl.when(slot[k] < len(NEAR))
        def _():
            tail_copy(k, near, 0).start()

        @pl.when(slot[k] >= len(NEAR))
        def _():
            tail_copy(k, far, len(NEAR)).start()

        count_copies[heads + k].start()
    for k in range(heads):
        head_copies[k].start()
        count_copies[k].start()

    def tile_of(k):
        return tiles[k].reshape(block, width)

    def scores_of(rounded, tile):
        return lax.dot_general(rounded, tile, (((1,), (1,)), ((), ())), preferred_element_type=jnp.float32)

    def dense_part(vector):
        return jnp.dot(vector, gram[...], precision=lax.Precision.HIGHEST, preferred_element_type=jnp.float32) + ridge_term * vector

    def apply_operator(vector):
        rounded = vector.astype(jnp.bfloat16)
        acc[...] = dense_part(vector)

        def some_tiles(i, carry):
            part = None
            for j in range(4):
                k = i * 4 + j
                tile = tile_of(k)
                scaled = (scores_of(rounded, tile) * weights[k]).astype(jnp.bfloat16)
                data = jnp.dot(scaled, tile, preferred_element_type=jnp.float32)
                part = data if part is None else part + data
            acc[...] += part
            return carry

        lax.fori_loop(0, total // 4, some_tiles, 0)
        return acc[...]

    solution = start[...]
    rounded = solution.astype(jnp.bfloat16)
    for copy in gram_copies:
        copy.wait()
    gram[...] = (halves[0].astype(jnp.float32) + halves[1].astype(jnp.float32)).reshape(width, width)
    acc[...] = -dense_part(solution)

    def first_tiles(first, i):
        part = None
        for j in range(2):
            k = first + i * 2 + j
            tile = tile_of(k)
            count = counts[k].astype(jnp.float32)
            weight = conf_alpha * count
            weights[k] = weight
            rated = jnp.where(count > 0.0, 1.0 + weight, 0.0).astype(jnp.bfloat16)
            scaled = (scores_of(rounded, tile) * weight).astype(jnp.bfloat16)
            data = jnp.dot(rated, tile, preferred_element_type=jnp.float32) - jnp.dot(
                scaled, tile, preferred_element_type=jnp.float32
            )
            part = data if part is None else part + data
        acc[...] += part

    def count_wait(k):
        pltpu.make_async_copy(head_counts.at[0, 0], counts.at[k], count_sems.at[k]).wait()

    def first_tails(i, carry):
        for j in range(2):
            k = i * 2 + j
            tail_copy(k, near, 0, True).wait()
            count_wait(heads + k)
        first_tiles(heads, i)
        return carry

    def first_heads(i, carry):
        for j in range(2):
            count_wait(i * 2 + j)
        first_tiles(0, i)
        return carry

    lax.fori_loop(0, tails // 2, first_tails, 0)
    for copy in head_copies:
        copy.wait()
    lax.fori_loop(0, heads // 2, first_heads, 0)
    residual = acc[...]
    direction = residual
    norm_now = jnp.sum(residual * residual, axis=1, keepdims=True)
    for turn_index in range(ITERS):
        image = apply_operator(direction)
        step_size = norm_now / (jnp.sum(direction * image, axis=1, keepdims=True) + epsilon)
        solution = solution + step_size * direction
        residual = residual - step_size * image
        if turn_index + 1 < ITERS:
            norm_next = jnp.sum(residual * residual, axis=1, keepdims=True)
            direction = residual + norm_next / (norm_now + epsilon) * direction
            norm_now = norm_next
    new_out[...] = solution
    res_out[...] = residual


def solve(slab, slot, user, start, near, far, same, other, head_counts, tail_counts):
    block, width = start.shape
    band = same.shape[2]
    total = head_counts.shape[1] + tail_counts.shape[1]
    out = jax.ShapeDtypeStruct((block, width), jnp.float32)
    return pl.pallas_call(
        solve_kernel,
        name="solve",
        grid_spec=pltpu.PrefetchScalarGridSpec(
            num_scalar_prefetch=3,
            grid=(1,),
            in_specs=[whole(start)] + [pl.BlockSpec(memory_space=pl.ANY)] * 6,
            out_specs=(whole(start), whole(start)),
            scratch_shapes=[
                pltpu.VMEM((total, USER, band, width), jnp.bfloat16),
                pltpu.VMEM((total, block, block), jnp.float32),
                pltpu.VMEM((total, block, block), jnp.int32),
                pltpu.VMEM((2, USER, width // USER, width), jnp.bfloat16),
                pltpu.VMEM((width, width), jnp.float32),
                pltpu.VMEM((block, width), jnp.float32),
                pltpu.SemaphoreType.DMA((total,)),
                pltpu.SemaphoreType.DMA((total,)),
                pltpu.SemaphoreType.DMA((USER,)),
                pltpu.SemaphoreType.DMA((USER,)),
            ],
        ),
        out_shape=(out, out),
    )(slab, slot, user.reshape(1), start, near, far, same, other, head_counts, tail_counts)


def ring(step, size=Z_SIZE):
    return [(i, (i + step) % size) for i in range(size)]


def line(step):
    return [(i, (i + 2 * step) % USER) for i in range(USER)]


def local(user_factors, item_factors, head_ids, tail_ids, head_counts, tail_counts):
    user, y, z = (lax.axis_index(axis) for axis in ALL)
    block_size = head_counts.shape[-1]
    width = item_factors.shape[1]
    per_shard = item_factors.shape[0] // block_size

    own = prepare(item_factors.reshape(per_shard, block_size, width), user)

    ids = tail_ids.reshape(-1)
    owner_of, local_of = ids // per_shard, ids % per_shard
    owners = jnp.arange(Y_SIZE * Z_SIZE, dtype=jnp.int32)
    requests = jnp.sum(jnp.where(owner_of[:, None] == owners[None, :], local_of[:, None], 0), axis=0)
    requests = jnp.tile(requests.reshape(Y_SIZE, Z_SIZE), (USER, 1))
    wanted = lax.all_to_all(requests, PLANE, 0, 0, tiled=True)

    up = down = own
    pieces = [own]
    near = None
    for turn in range(1, 4):
        up = lax.ppermute(up, "z", ring(1))
        down = lax.ppermute(down, "z", ring(-1))
        pieces += [up, down]
        if turn == 1:
            served_near = pick_near(wanted, z, pieces)
            near = lax.all_to_all(served_near, PLANE, 0, 0, tiled=True)
    pieces.append(lax.ppermute(up, "z", ring(1)))
    served_far, shared = pick_far(wanted, head_ids, z, pieces)
    far = lax.all_to_all(served_far, PLANE, 0, 0, tiled=True)
    slabs = [shared] + [lax.ppermute(shared, "y", ring(-step, Y_SIZE)) for step in range(1, Y_SIZE)]
    merged = merge(head_ids // (per_shard * Z_SIZE), y, slabs)
    same = jnp.stack([merged] + [lax.ppermute(merged, "user", line(-step)) for step in range(1, USER // 2)])
    other = lax.ppermute(same, "user", [(i, i ^ 1) for i in range(USER)])

    slot = jnp.asarray(SLOT_OF_SHIFT, jnp.int32)[(owner_of - z) % Z_SIZE]
    near = near.reshape(USER, Y_SIZE, *near.shape[1:])
    far = far.reshape(USER, Y_SIZE, *far.shape[1:])
    return solve(owner_of // Z_SIZE, slot, user, user_factors, near, far, same, other, head_counts, tail_counts)


def solution(mesh):
    fine = Mesh(mesh.devices.reshape(USER, Y_SIZE, Z_SIZE), ALL)
    return jax.shard_map(
        local,
        mesh=fine,
        in_specs=(P(ALL, None), P(("y", "z"), None), P(), P(ALL, None), P(ALL, None, None, None), P(ALL, None, None, None)),
        out_specs=(P(ALL, None), P(ALL, None)),
        check_vma=False,
    )
```

```python
import functools

import jax
import jax.numpy as jnp
from jax import lax
from jax.experimental import pallas as pl
from jax.experimental.pallas import tpu as pltpu
from jax.sharding import Mesh, PartitionSpec as P

ITERS = 2

conf_alpha = 4.0
ridge_term = 0.1
epsilon = 1e-06

USER, Y_SIZE, Z_SIZE = 8, 4, 8
ALL = ("user", "y", "z")
PLANE = ("user", "y")
PARTS = ((0, -1, 1), (-2, 2), (-3, 3, 4))
OFFSETS = sum(PARTS, ())
FIRST = tuple(sum(len(part) for part in PARTS[:n]) for n in range(len(PARTS)))
SLOT_OF_SHIFT = tuple(OFFSETS.index(s if s <= 4 else s - 8) for s in range(8))


MIB = 1 << 20
IN_VMEM = pl.BlockSpec(memory_space=pltpu.VMEM)


def limit(mib):
    return pltpu.CompilerParams(vmem_limit_bytes=mib * MIB)


def bf16(*shape):
    return jax.ShapeDtypeStruct(shape, jnp.bfloat16)


def store_split(out, at, values):
    high = values.astype(jnp.bfloat16)
    out[at] = high
    out[at + 1] = (values - high.astype(jnp.float32)).astype(jnp.bfloat16)


def prepare_kernel(place, blocks, out, gram):
    total, block, width = blocks.shape
    band = block // USER
    row = pl.multiple_of(place[0] * band, band)
    for k in range(total):
        rows = blocks[k]
        part = lax.dot_general(rows, rows, (((0,), (0,)), ((), ())), preferred_element_type=jnp.float32)
        if k == 0:
            gram[...] = part
        else:
            gram[...] += part
        out[k] = blocks[k, pl.ds(row, band), :]
    store_split(out, total, gram[pl.ds(row, width // USER), :])


def prepare(blocks, user):
    total, block, width = blocks.shape
    out = bf16(total + 2, block // USER, width)
    return pl.pallas_call(
        prepare_kernel,
        name="prepare",
        grid_spec=pltpu.PrefetchScalarGridSpec(
            num_scalar_prefetch=1,
            in_specs=[IN_VMEM],
            out_specs=IN_VMEM,
            scratch_shapes=[pltpu.VMEM((width, width), jnp.float32)],
        ),
        compiler_params=limit(8),
        out_shape=out,
    )(user.reshape(1), blocks)


def pick_kernel(offsets, wanted, place, *refs):
    pieces, out = refs[:-1], refs[-1]
    z = place[0]
    band = pieces[0].shape[1]
    for p in range(out.shape[0]):
        for slot, (source, offset) in enumerate(zip(pieces, offsets)):
            out[p, slot * band : (slot + 1) * band, :] = source[wanted[p, (z + offset) & (Z_SIZE - 1)]]


def pick(offsets, wanted, z, pieces):
    _, band, width = pieces[0].shape
    out = bf16(wanted.shape[0], len(offsets) * band, width)
    return pl.pallas_call(
        functools.partial(pick_kernel, offsets),
        name="pick",
        grid_spec=pltpu.PrefetchScalarGridSpec(
            num_scalar_prefetch=2,
            in_specs=[IN_VMEM] * len(pieces),
            out_specs=IN_VMEM,
        ),
        compiler_params=limit(4),
        out_shape=out,
    )(wanted, z.reshape(1), *pieces)


def gather_heads_kernel(head_ids, place, *refs):
    pieces, out = refs[:-1], refs[-1]
    total, band, width = pieces[0].shape
    per_shard = total - 2
    heads = head_ids.shape[0]
    for h in range(heads):
        block = head_ids[h]
        shift = (block // per_shard - place[0]) & (Z_SIZE - 1)
        for source, offset in zip(pieces, OFFSETS):

            @pl.when(shift == offset % Z_SIZE)
            def _():
                out[h] = source[block & (per_shard - 1)]

    gram = jnp.zeros((band, width), jnp.float32)
    for source in pieces:
        gram += source[per_shard].astype(jnp.float32) + source[per_shard + 1].astype(jnp.float32)
    store_split(out, heads, gram)


def gather_heads(head_ids, z, pieces):
    out = bf16(head_ids.shape[0] + 2, *pieces[0].shape[1:])
    return pl.pallas_call(
        gather_heads_kernel,
        name="gather_heads",
        grid_spec=pltpu.PrefetchScalarGridSpec(
            num_scalar_prefetch=2,
            in_specs=[IN_VMEM] * len(pieces),
            out_specs=IN_VMEM,
        ),
        compiler_params=limit(4),
        out_shape=out,
    )(head_ids, z.reshape(1), *pieces)


def merge_kernel(slabs, place, own, above, across, below, out):
    heads = slabs.shape[0]
    pieces = (own, above, across, below)
    for h in range(heads):
        shift = (slabs[h] - place[0]) & (Y_SIZE - 1)
        for other, source in enumerate(pieces):

            @pl.when(shift == other)
            def _():
                out[h] = source[h]

    gram = jnp.zeros(out.shape[1:], jnp.float32)
    for source in pieces:
        gram += source[heads].astype(jnp.float32) + source[heads + 1].astype(jnp.float32)
    store_split(out, heads, gram)


def merge(slabs, y, pieces):
    return pl.pallas_call(
        merge_kernel,
        name="merge",
        grid_spec=pltpu.PrefetchScalarGridSpec(
            num_scalar_prefetch=2,
            in_specs=[IN_VMEM] * len(pieces),
            out_specs=IN_VMEM,
        ),
        compiler_params=limit(4),
        out_shape=bf16(*pieces[0].shape),
    )(slabs, y.reshape(1), *pieces)


def weigh_kernel(head_counts, tail_counts, weights, counts, sems):
    heads, tails = head_counts.shape[1], tail_counts.shape[1]
    block = weights.shape[0]
    copies = [pltpu.make_async_copy(head_counts.at[0, k], counts.at[k], sems.at[k]) for k in range(heads)]
    copies += [pltpu.make_async_copy(tail_counts.at[0, k], counts.at[heads + k], sems.at[heads + k]) for k in range(tails)]
    for copy in copies:
        copy.start()

    def one_tile(k, carry):
        pltpu.make_async_copy(head_counts.at[0, 0], counts.at[k], sems.at[k]).wait()
        weight = conf_alpha * counts[k].astype(jnp.float32)
        weights[:, pl.ds(pl.multiple_of(k * block, block), block)] = weight.astype(jnp.bfloat16)
        return carry

    lax.fori_loop(0, heads + tails, one_tile, 0)


def weigh(head_counts, tail_counts):
    total, block = head_counts.shape[1] + tail_counts.shape[1], head_counts.shape[-1]
    return pl.pallas_call(
        weigh_kernel,
        name="weigh",
        in_specs=[pl.BlockSpec(memory_space=pltpu.HBM)] * 2,
        out_specs=IN_VMEM,
        out_shape=bf16(block, total * block),
        scratch_shapes=[pltpu.VMEM((total, block, block), jnp.int32), pltpu.SemaphoreType.DMA((total,))],
        compiler_params=limit(63),
    )(head_counts, tail_counts)


def solve_kernel(slab, slot, place, start, *refs):
    served, refs = refs[: len(PARTS)], refs[len(PARTS) :]
    same, other, weights_in, new_out, res_out, *refs = refs
    weights, tiles, scaled, gram, acc, tile_sems, gram_sems, head_sems, weight_sems = refs
    block, width = start.shape
    total = weights.shape[1] // block
    heads = same.shape[1] - 2
    tails = total - heads
    band = same.shape[2]

    gram_copies, head_copies = [], []
    x, core = place[0] // 2, place[0] % 2
    for i, source in enumerate((same, other)):
        for j in range(USER // 2):
            n = i * (USER // 2) + j
            user = ((x + j) & (USER // 2 - 1)) * 2 + (core if i == 0 else 1 - core)
            gram_copies.append(pltpu.make_async_copy(source.at[j, heads:], gram.at[:, user], gram_sems.at[n]))
            head_copies.append(pltpu.make_async_copy(source.at[j, :heads], tiles.at[:heads, user], head_sems.at[n]))

    chunk = weights.shape[1] // weight_sems.shape[0]
    weight_copies = [
        pltpu.make_async_copy(weights_in.at[:, pl.ds(n * chunk, chunk)], weights.at[:, pl.ds(n * chunk, chunk)], weight_sems.at[n])
        for n in range(weight_sems.shape[0])
    ]

    def tail_copy(k, part, any_rows=False):
        row = 0 if any_rows else pl.multiple_of((slot[k] - FIRST[part]) * band, band)
        return pltpu.make_async_copy(
            served[part].at[:, 0 if any_rows else slab[k], pl.ds(row, band), :], tiles.at[heads + k], tile_sems.at[heads + k]
        )

    for copy in gram_copies:
        copy.start()
    for copy in head_copies + weight_copies:
        copy.start()
    for k in range(tails):
        for part, offsets in enumerate(PARTS):

            @pl.when((slot[k] >= FIRST[part]) & (slot[k] < FIRST[part] + len(offsets)))
            def _():
                tail_copy(k, part).start()

    def tile_of(k):
        return tiles[k].reshape(block, width)

    def columns(k, count=1):
        return pl.ds(pl.multiple_of(k * block, block), count * block)

    def scores_of(rounded, tile):
        return lax.dot_general(rounded, tile, (((1,), (1,)), ((), ())), preferred_element_type=jnp.float32)

    def matmul(left, right):
        return jnp.dot(left, right, preferred_element_type=jnp.float32)

    def dense_part(vector, high):
        low = (vector - high.astype(jnp.float32)).astype(jnp.bfloat16)
        gram_high, gram_low = gram[0].reshape(width, width), gram[1].reshape(width, width)
        return matmul(high, gram_high) + (matmul(high, gram_low) + matmul(low, gram_high)) + ridge_term * vector

    def data_part(left, group):
        def some(i, carry):
            k = i * group
            rows = tiles[pl.ds(k, group)].reshape(group * block, width)
            acc[...] += matmul(left(columns(k, group)), rows)
            return carry

        lax.fori_loop(0, total // group, some, 0)

    def scores_part(rounded, first, count, wait=False):
        def some(i, carry):
            if wait:
                for j in range(4):
                    tail_copy(i * 4 + j, 0, True).wait()
            for j in range(4):
                k = first + i * 4 + j
                weight = weights[:, columns(k)].astype(jnp.float32)
                scaled[:, columns(k)] = (scores_of(rounded, tile_of(k)) * weight).astype(jnp.bfloat16)
            return carry

        lax.fori_loop(0, count // 4, some, 0)

    def apply_operator(vector):
        rounded = vector.astype(jnp.bfloat16)
        acc[...] = dense_part(vector, rounded)
        scores_part(rounded, 0, total)
        data_part(lambda at: scaled[:, at], 6)
        return acc[...]

    solution = start[...]
    rounded = solution.astype(jnp.bfloat16)

    def rated(at):
        weight = weights[:, at]
        return jnp.where(weight > 0, weight + 1, jnp.zeros_like(weight))

    for copy in gram_copies + head_copies + weight_copies:
        copy.wait()
    acc[...] = dense_part(solution, rounded)
    scores_part(rounded, 0, heads)
    scores_part(rounded, heads, tails, True)
    data_part(lambda at: scaled[:, at], 6)
    acc[...] = -acc[...]
    data_part(rated, 6)
    residual = acc[...]
    direction = residual
    norm_now = jnp.sum(residual * residual, axis=1, keepdims=True)
    for turn_index in range(ITERS):
        image = apply_operator(direction)
        step_size = norm_now / (jnp.sum(direction * image, axis=1, keepdims=True) + epsilon)
        solution = solution + step_size * direction
        residual = residual - step_size * image
        if turn_index + 1 < ITERS:
            norm_next = jnp.sum(residual * residual, axis=1, keepdims=True)
            direction = residual + norm_next / (norm_now + epsilon) * direction
            norm_now = norm_next
    new_out[...] = solution
    res_out[...] = residual


def solve(slab, slot, user, start, served, same, other, weights):
    block, width = start.shape
    band = same.shape[2]
    total = weights.shape[1] // block
    out = jax.ShapeDtypeStruct((block, width), jnp.float32)
    return pl.pallas_call(
        solve_kernel,
        name="solve",
        grid_spec=pltpu.PrefetchScalarGridSpec(
            num_scalar_prefetch=3,
            in_specs=[IN_VMEM] + [pl.BlockSpec(memory_space=pltpu.HBM)] * (len(served) + 3),
            out_specs=(IN_VMEM, IN_VMEM),
            scratch_shapes=[
                pltpu.VMEM((block, total * block), jnp.bfloat16),
                pltpu.VMEM((total, USER, band, width), jnp.bfloat16),
                pltpu.VMEM((block, total * block), jnp.bfloat16),
                pltpu.VMEM((2, USER, width // USER, width), jnp.bfloat16),
                pltpu.VMEM((block, width), jnp.float32),
                pltpu.SemaphoreType.DMA((total,)),
                pltpu.SemaphoreType.DMA((USER,)),
                pltpu.SemaphoreType.DMA((USER,)),
                pltpu.SemaphoreType.DMA((4,)),
            ],
        ),
        out_shape=(out, out),
        compiler_params=limit(63),
    )(slab, slot, user.reshape(1), start, *served, same, other, weights)


def ring(step, size=Z_SIZE):
    return [(i, (i + step) % size) for i in range(size)]


def line(step):
    return [(i, (i + 2 * step) % USER) for i in range(USER)]


def local(user_factors, item_factors, head_ids, tail_ids, head_counts, tail_counts):
    user, y, z = (lax.axis_index(axis) for axis in ALL)
    block_size = head_counts.shape[-1]
    width = item_factors.shape[1]
    per_shard = item_factors.shape[0] // block_size

    own = prepare(item_factors.reshape(per_shard, block_size, width), user)

    ids = tail_ids.reshape(-1)
    owner_of, local_of = ids // per_shard, ids % per_shard
    owners = jnp.arange(Y_SIZE * Z_SIZE, dtype=jnp.int32)
    requests = jnp.sum(jnp.where(owner_of[:, None] == owners[None, :], local_of[:, None], 0), axis=0)
    requests = jnp.tile(requests.reshape(Y_SIZE, Z_SIZE), (USER, 1))
    wanted = lax.all_to_all(requests, PLANE, 0, 0, tiled=True)

    up = down = own
    pieces = [own]
    for _ in range(1, 4):
        up = lax.ppermute(up, "z", ring(1))
        down = lax.ppermute(down, "z", ring(-1))
        pieces += [up, down]
    pieces.append(lax.ppermute(up, "z", ring(1)))

    served = []
    for part, offsets in enumerate(PARTS):
        picked = pick(offsets, wanted, z, pieces[FIRST[part] : FIRST[part] + len(offsets)])
        arrived = lax.all_to_all(picked, PLANE, 0, 0, tiled=True)
        served.append(arrived.reshape(USER, Y_SIZE, *arrived.shape[1:]))

    shared = gather_heads(head_ids, z, pieces)
    slabs = [shared] + [lax.ppermute(shared, "y", ring(-step, Y_SIZE)) for step in range(1, Y_SIZE)]
    merged = merge(head_ids // (per_shard * Z_SIZE), y, slabs)
    same = jnp.stack([merged] + [lax.ppermute(merged, "user", line(-step)) for step in range(1, USER // 2)])
    other = lax.ppermute(same, "user", [(i, i ^ 1) for i in range(USER)])

    weights = weigh(head_counts, tail_counts)
    slot = jnp.asarray(SLOT_OF_SHIFT, jnp.int32)[(owner_of - z) % Z_SIZE]
    return solve(owner_of // Z_SIZE, slot, user, user_factors, served, same, other, weights)


def solution(mesh):
    fine = Mesh(mesh.devices.reshape(USER, Y_SIZE, Z_SIZE), ALL)
    return jax.shard_map(
        local,
        mesh=fine,
        in_specs=(P(ALL, None), P(("y", "z"), None), P(), P(ALL, None), P(ALL, None, None, None), P(ALL, None, None, None)),
        out_specs=(P(ALL, None), P(ALL, None)),
        check_vma=False,
    )
```

```python
import functools

import jax
import jax.numpy as jnp
from jax import lax
from jax.experimental import pallas as pl
from jax.experimental.pallas import tpu as pltpu
from jax.sharding import Mesh, PartitionSpec as P

ITERS = 2

conf_alpha = 4.0
ridge_term = 0.1
epsilon = 1e-06

USER, Y_SIZE, Z_SIZE = 8, 4, 8
ALL = ("user", "y", "z")
PLANE = ("user", "y")
PARTS = ((0, -1, 1), (-2, 2), (-3, 3, 4))
OFFSETS = sum(PARTS, ())
FIRST = tuple(sum(len(part) for part in PARTS[:n]) for n in range(len(PARTS)))
SLOT_OF_SHIFT = tuple(OFFSETS.index(s if s <= 4 else s - 8) for s in range(8))


MIB = 1 << 20
IN_VMEM = pl.BlockSpec(memory_space=pltpu.VMEM)


def limit(mib):
    return pltpu.CompilerParams(vmem_limit_bytes=mib * MIB)


def bf16(*shape):
    return jax.ShapeDtypeStruct(shape, jnp.bfloat16)


def store_split(out, at, values):
    high = values.astype(jnp.bfloat16)
    out[at] = high
    out[at + 1] = (values - high.astype(jnp.float32)).astype(jnp.bfloat16)


def prepare_kernel(place, blocks, out, gram):
    total, block, width = blocks.shape
    band = block // USER
    row = pl.multiple_of(place[0] * band, band)
    for k in range(total):
        rows = blocks[k]
        part = lax.dot_general(rows, rows, (((0,), (0,)), ((), ())), preferred_element_type=jnp.float32)
        if k == 0:
            gram[...] = part
        else:
            gram[...] += part
        out[k] = blocks[k, pl.ds(row, band), :]
    store_split(out, total, gram[pl.ds(row, width // USER), :])


def prepare(blocks, user):
    total, block, width = blocks.shape
    out = bf16(total + 2, block // USER, width)
    return pl.pallas_call(
        prepare_kernel,
        name="prepare",
        grid_spec=pltpu.PrefetchScalarGridSpec(
            num_scalar_prefetch=1,
            in_specs=[IN_VMEM],
            out_specs=IN_VMEM,
            scratch_shapes=[pltpu.VMEM((width, width), jnp.float32)],
        ),
        compiler_params=limit(8),
        out_shape=out,
    )(user.reshape(1), blocks)


def pick_kernel(offsets, wanted, place, *refs):
    pieces, out = refs[:-1], refs[-1]
    z = place[0]
    band = pieces[0].shape[1]
    for p in range(out.shape[0]):
        for slot, (source, offset) in enumerate(zip(pieces, offsets)):
            out[p, slot * band : (slot + 1) * band, :] = source[wanted[p, (z + offset) & (Z_SIZE - 1)]]


def pick(offsets, wanted, z, pieces):
    _, band, width = pieces[0].shape
    out = bf16(wanted.shape[0], len(offsets) * band, width)
    return pl.pallas_call(
        functools.partial(pick_kernel, offsets),
        name="pick",
        grid_spec=pltpu.PrefetchScalarGridSpec(
            num_scalar_prefetch=2,
            in_specs=[IN_VMEM] * len(pieces),
            out_specs=IN_VMEM,
        ),
        compiler_params=limit(4),
        out_shape=out,
    )(wanted, z.reshape(1), *pieces)


def gather_heads_kernel(head_ids, place, *refs):
    pieces, out = refs[:-1], refs[-1]
    total, band, width = pieces[0].shape
    per_shard = total - 2
    heads = head_ids.shape[0]
    for h in range(heads):
        block = head_ids[h]
        shift = (block // per_shard - place[0]) & (Z_SIZE - 1)
        for source, offset in zip(pieces, OFFSETS):

            @pl.when(shift == offset % Z_SIZE)
            def _():
                out[h] = source[block & (per_shard - 1)]

    gram = jnp.zeros((band, width), jnp.float32)
    for source in pieces:
        gram += source[per_shard].astype(jnp.float32) + source[per_shard + 1].astype(jnp.float32)
    store_split(out, heads, gram)


def gather_heads(head_ids, z, pieces):
    out = bf16(head_ids.shape[0] + 2, *pieces[0].shape[1:])
    return pl.pallas_call(
        gather_heads_kernel,
        name="gather_heads",
        grid_spec=pltpu.PrefetchScalarGridSpec(
            num_scalar_prefetch=2,
            in_specs=[IN_VMEM] * len(pieces),
            out_specs=IN_VMEM,
        ),
        compiler_params=limit(4),
        out_shape=out,
    )(head_ids, z.reshape(1), *pieces)


def merge_kernel(slabs, place, own, above, across, below, out):
    heads = slabs.shape[0]
    pieces = (own, above, across, below)
    for h in range(heads):
        shift = (slabs[h] - place[0]) & (Y_SIZE - 1)
        for other, source in enumerate(pieces):

            @pl.when(shift == other)
            def _():
                out[h] = source[h]

    gram = jnp.zeros(out.shape[1:], jnp.float32)
    for source in pieces:
        gram += source[heads].astype(jnp.float32) + source[heads + 1].astype(jnp.float32)
    store_split(out, heads, gram)


def merge(slabs, y, pieces):
    return pl.pallas_call(
        merge_kernel,
        name="merge",
        grid_spec=pltpu.PrefetchScalarGridSpec(
            num_scalar_prefetch=2,
            in_specs=[IN_VMEM] * len(pieces),
            out_specs=IN_VMEM,
        ),
        compiler_params=limit(4),
        out_shape=bf16(*pieces[0].shape),
    )(slabs, y.reshape(1), *pieces)


def matmul(left, right):
    return jnp.dot(left, right, preferred_element_type=jnp.float32)


def scores_of(rounded, tile):
    return lax.dot_general(rounded, tile, (((1,), (1,)), ((), ())), preferred_element_type=jnp.float32)


def dense_part(vector, high, gram):
    low = (vector - high.astype(jnp.float32)).astype(jnp.bfloat16)
    width = vector.shape[1]
    gram_high, gram_low = gram[0].reshape(width, width), gram[1].reshape(width, width)
    return matmul(high, gram_high) + (matmul(high, gram_low) + matmul(low, gram_high)) + ridge_term * vector


def columns(k, block, count=1):
    return pl.ds(pl.multiple_of(k * block, block), count * block)


def first_pass(acc, rounded, tiles, weights, first, pairs):
    block = rounded.shape[0]

    def some(i, carry):
        part = None
        for j in range(2):
            k = first + i * 2 + j
            tile = tiles[k].reshape(block, -1)
            weight = weights[:, columns(k, block)]
            rated = jnp.where(weight > 0, weight + 1, jnp.zeros_like(weight))
            scaled = (scores_of(rounded, tile) * -weight.astype(jnp.float32)).astype(jnp.bfloat16)
            data = matmul(rated, tile) + matmul(scaled, tile)
            part = data if part is None else part + data
        acc[...] += part
        return carry

    lax.fori_loop(0, pairs, some, 0)


def warm_kernel(order, slab, slot, early, place, start, *refs):
    served, refs = refs[: len(PARTS) - 1], refs[len(PARTS) - 1 :]
    same, other, head_counts, tail_counts, weights, tiles, gram, partial, *refs = refs
    counts, count_sems, tile_sems, gram_sems, head_sems = refs
    heads, tails = head_counts.shape[1], tail_counts.shape[1]
    block = start.shape[0]
    band = same.shape[2]

    gram_copies, head_copies = [], []
    x, core = place[0] // 2, place[0] % 2
    for i, source in enumerate((same, other)):
        for j in range(USER // 2):
            n = i * (USER // 2) + j
            user = ((x + j) & (USER // 2 - 1)) * 2 + (core if i == 0 else 1 - core)
            gram_copies.append(pltpu.make_async_copy(source.at[j, heads:], gram.at[:, user], gram_sems.at[n]))
            head_copies.append(pltpu.make_async_copy(source.at[j, :heads], tiles.at[:heads, user], head_sems.at[n]))
    count_copies = [pltpu.make_async_copy(head_counts.at[0, k], counts.at[k], count_sems.at[k]) for k in range(heads)]
    count_copies += [
        pltpu.make_async_copy(tail_counts.at[0, order[k]], counts.at[heads + k], count_sems.at[heads + k])
        for k in range(tails)
    ]

    def tail_copy(k, part):
        row = pl.multiple_of((slot[k] - FIRST[part]) * band, band)
        return pltpu.make_async_copy(
            served[part].at[:, slab[k], pl.ds(row, band), :], tiles.at[heads + k], tile_sems.at[k]
        )

    for copy in gram_copies + head_copies + count_copies:
        copy.start()
    for k in range(tails):
        for part in range(len(PARTS) - 1):

            @pl.when((slot[k] >= FIRST[part]) & (slot[k] < FIRST[part + 1]))
            def _():
                tail_copy(k, part).start()

    def one_tile(k, carry):
        pltpu.make_async_copy(head_counts.at[0, 0], counts.at[k], count_sems.at[k]).wait()
        weights[:, columns(k, block)] = (conf_alpha * counts[k].astype(jnp.float32)).astype(jnp.bfloat16)
        return carry

    lax.fori_loop(0, heads + tails, one_tile, 0)
    for copy in gram_copies + head_copies:
        copy.wait()
    for k in range(tails):

        @pl.when(slot[k] < FIRST[-1])
        def _():
            pltpu.make_async_copy(served[0].at[:, 0, pl.ds(0, band), :], tiles.at[heads + k], tile_sems.at[k]).wait()

    vector = start[...]
    rounded = vector.astype(jnp.bfloat16)
    partial[...] = -dense_part(vector, rounded, gram)
    first_pass(partial, rounded, tiles, weights, 0, (heads + early[0]) // 2)


def warm(sorted_tails, user, start, served, same, other, head_counts, tail_counts):
    block, width = start.shape
    band = same.shape[2]
    heads, tails = head_counts.shape[1], tail_counts.shape[1]
    total = heads + tails
    return pl.pallas_call(
        warm_kernel,
        name="warm",
        grid_spec=pltpu.PrefetchScalarGridSpec(
            num_scalar_prefetch=5,
            in_specs=[IN_VMEM] + [pl.BlockSpec(memory_space=pl.ANY)] * (len(served) + 4),
            out_specs=(IN_VMEM,) * 4,
            scratch_shapes=[
                pltpu.VMEM((total, block, block), jnp.int32),
                pltpu.SemaphoreType.DMA((total,)),
                pltpu.SemaphoreType.DMA((tails,)),
                pltpu.SemaphoreType.DMA((USER,)),
                pltpu.SemaphoreType.DMA((USER,)),
            ],
        ),
        out_shape=(
            bf16(block, total * block),
            bf16(total, USER, band, width),
            bf16(2, USER, width // USER, width),
            jax.ShapeDtypeStruct((block, width), jnp.float32),
        ),
        compiler_params=limit(63),
    )(*sorted_tails, user.reshape(1), start, *served, same, other, head_counts, tail_counts)


def solve_kernel(slab, slot, early, start, weights_in, tiles_in, gram_in, partial, served, new_out, res_out, *refs):
    weights, tiles, gram, acc, scaled, weight_sems, tile_sems, small_sems = refs
    block, width = start.shape
    total = tiles.shape[0]
    tails = slab.shape[0]
    heads = total - tails
    band = tiles.shape[2]

    small_copies = [pltpu.make_async_copy(partial, acc, small_sems.at[0]), pltpu.make_async_copy(gram_in, gram, small_sems.at[1])]
    chunks = weight_sems.shape[0]
    chunk = weights.shape[1] // chunks
    weight_copies = [
        pltpu.make_async_copy(weights_in.at[:, n * chunk : (n + 1) * chunk], weights.at[:, n * chunk : (n + 1) * chunk], weight_sems.at[n])
        for n in range(chunks)
    ]

    def early_copy(k):
        return pltpu.make_async_copy(tiles_in.at[k], tiles.at[k], tile_sems.at[k])

    def late_copy(k):
        row = pl.multiple_of((slot[k] - FIRST[-1]) * band, band)
        return pltpu.make_async_copy(
            served.at[:, slab[k], pl.ds(row, band), :], tiles.at[heads + k], tile_sems.at[heads + k]
        )

    small_copies[0].start()
    for k in reversed(range(tails)):

        @pl.when(slot[k] >= FIRST[-1])
        def _():
            late_copy(k).start()

    for copy in reversed(weight_copies):
        copy.start()
    small_copies[1].start()
    for k in range(heads):
        early_copy(k).start()
    for k in range(tails):

        @pl.when(slot[k] < FIRST[-1])
        def _():
            early_copy(heads + k).start()

    def tile_wait(k, carry):
        pltpu.make_async_copy(tiles_in.at[0], tiles.at[k], tile_sems.at[k]).wait()
        return carry

    def apply_operator(vector):
        rounded = vector.astype(jnp.bfloat16)
        acc[...] = dense_part(vector, rounded, gram)

        def some_scores(i, carry):
            for j in range(4):
                k = i * 4 + j
                weight = weights[:, columns(k, block)].astype(jnp.float32)
                scores = scores_of(rounded, tiles[k].reshape(block, width))
                scaled[:, columns(k, block)] = (scores * weight).astype(jnp.bfloat16)
            return carry

        def some_data(i, carry):
            k = i * 6
            acc[...] += matmul(scaled[:, columns(k, block, 6)], tiles[pl.ds(k, 6)].reshape(6 * block, width))
            return carry

        lax.fori_loop(0, total // 4, some_scores, 0)
        lax.fori_loop(0, total // 6, some_data, 0)
        return acc[...]

    solution = start[...]
    lax.fori_loop(heads + early[0], total, tile_wait, 0)
    for copy in reversed(weight_copies):
        copy.wait()
    small_copies[0].wait()
    first_pass(acc, solution.astype(jnp.bfloat16), tiles, weights, heads + early[0], (tails - early[0]) // 2)
    lax.fori_loop(0, heads + early[0], tile_wait, 0)
    small_copies[1].wait()
    residual = acc[...]
    direction = residual
    norm_now = jnp.sum(residual * residual, axis=1, keepdims=True)
    for turn_index in range(ITERS):
        image = apply_operator(direction)
        step_size = norm_now / (jnp.sum(direction * image, axis=1, keepdims=True) + epsilon)
        solution = solution + step_size * direction
        residual = residual - step_size * image
        if turn_index + 1 < ITERS:
            norm_next = jnp.sum(residual * residual, axis=1, keepdims=True)
            direction = residual + norm_next / (norm_now + epsilon) * direction
            norm_now = norm_next
    new_out[...] = solution
    res_out[...] = residual


def solve(slab, slot, early, start, warmed, served):
    block, width = start.shape
    weights, tiles = warmed[:2]
    out = jax.ShapeDtypeStruct((block, width), jnp.float32)
    return pl.pallas_call(
        solve_kernel,
        name="solve",
        grid_spec=pltpu.PrefetchScalarGridSpec(
            num_scalar_prefetch=3,
            in_specs=[IN_VMEM] + [pl.BlockSpec(memory_space=pl.ANY)] * (1 + len(warmed)),
            out_specs=(IN_VMEM, IN_VMEM),
            scratch_shapes=[pltpu.VMEM(array.shape, array.dtype) for array in warmed]
            + [
                pltpu.VMEM(weights.shape, jnp.bfloat16),
                pltpu.SemaphoreType.DMA((4,)),
                pltpu.SemaphoreType.DMA((tiles.shape[0],)),
                pltpu.SemaphoreType.DMA((2,)),
            ],
        ),
        out_shape=(out, out),
        compiler_params=limit(63),
    )(slab, slot, early, start, *warmed, served)


def ring(step, size=Z_SIZE):
    return [(i, (i + step) % size) for i in range(size)]


def line(step):
    return [(i, (i + 2 * step) % USER) for i in range(USER)]


def local(user_factors, item_factors, head_ids, tail_ids, head_counts, tail_counts):
    user, y, z = (lax.axis_index(axis) for axis in ALL)
    block_size = head_counts.shape[-1]
    width = item_factors.shape[1]
    per_shard = item_factors.shape[0] // block_size

    own = prepare(item_factors.reshape(per_shard, block_size, width), user)

    ids = tail_ids.reshape(-1)
    owner_of, local_of = ids // per_shard, ids % per_shard
    owners = jnp.arange(Y_SIZE * Z_SIZE, dtype=jnp.int32)
    requests = jnp.sum(jnp.where(owner_of[:, None] == owners[None, :], local_of[:, None], 0), axis=0)
    requests = jnp.tile(requests.reshape(Y_SIZE, Z_SIZE), (USER, 1))
    wanted = lax.all_to_all(requests, PLANE, 0, 0, tiled=True)

    up = down = own
    pieces = [own]
    for _ in range(1, 4):
        up = lax.ppermute(up, "z", ring(1))
        down = lax.ppermute(down, "z", ring(-1))
        pieces += [up, down]
    pieces.append(lax.ppermute(up, "z", ring(1)))

    served = []
    for part, offsets in enumerate(PARTS):
        picked = pick(offsets, wanted, z, pieces[FIRST[part] : FIRST[part] + len(offsets)])
        arrived = lax.all_to_all(picked, PLANE, 0, 0, tiled=True)
        served.append(arrived.reshape(USER, Y_SIZE, *arrived.shape[1:]))

    shared = gather_heads(head_ids, z, pieces)
    slabs = [shared]
    for step in range(1, Y_SIZE):
        slabs.append(lax.ppermute(shared, "y", ring(-step, Y_SIZE)))
    merged = merge(head_ids // (per_shard * Z_SIZE), y, slabs)
    same = [merged]
    for step in range(1, USER // 2):
        same.append(lax.ppermute(merged, "user", line(-step)))
    same = jnp.stack(same)
    other = lax.ppermute(same, "user", [(i, i ^ 1) for i in range(USER)])

    slot = jnp.asarray(SLOT_OF_SHIFT, jnp.int32)[(owner_of - z) % Z_SIZE]
    late = slot >= FIRST[-1]
    index = jnp.arange(slot.shape[0], dtype=jnp.int32)
    before = (index[None, :] < index[:, None]) | (late[:, None] & ~late[None, :])
    before &= ~(late[None, :] & ~late[:, None])
    place = jnp.sum(before.astype(jnp.int32), axis=1)
    table = place[:, None] == index[None, :]
    order, slab, slot = (
        jnp.sum(jnp.where(table, values[:, None], 0), axis=0) for values in (index, owner_of // Z_SIZE, slot)
    )
    early = (jnp.sum((~late).astype(jnp.int32)) & -2).reshape(1)
    warmed = warm((order, slab, slot, early), user, user_factors, served[:-1], same, other, head_counts, tail_counts)
    return solve(slab, slot, early, user_factors, warmed, served[-1])


def solution(mesh):
    fine = Mesh(mesh.devices.reshape(USER, Y_SIZE, Z_SIZE), ALL)
    return jax.shard_map(
        local,
        mesh=fine,
        in_specs=(P(ALL, None), P(("y", "z"), None), P(), P(ALL, None), P(ALL, None, None, None), P(ALL, None, None, None)),
        out_specs=(P(ALL, None), P(ALL, None)),
        check_vma=False,
    )
```
